256 devices in a mesh: mode: 4 (over z_lo), space: 64 (over x, y, z_hi, core).
Axes of the slice: x: 4, y: 4, z: 8 (z_hi: 2, z_lo: 4; z = z_hi * 4 + z_lo), core: 2. Of those that a mesh axis runs over, the one named last changes fastest.
Arguments:
- traces: float32 [120, 196608], P('mode', 'space'), may hold values from -6 to 6
- elem_mats: float32 [5, 36, 65536], P(None, None, 'space'), may hold values from -1.8 to 1.8
- face_links: int32 [6, 65536], P(None, 'space'), may hold values from 0 to 4095
- pair_modes: int32 [2, 1440], replicated, may hold values from 0 to 119
- pair_terms: int32 [1440], replicated, may hold values from 0 to 3
- pair_values: float32 [1440], replicated, may hold values from -3 to 3
Outputs:
- applied: float32 [120, 196608], P('mode', 'space')
The draws below stay inside these ranges and needn't reach their ends.
Inputs may be any that keep to these rules, and one draw needn't show every extreme that they name: `face_links`: indices into an element's subdomain's 3072 faces preceded and followed by 512 faces of the neighbouring subdomains.
All inputs are finite; a program needn't handle non-finite values.
Results may differ from the reference program's by a relative error of at most 0.0001.
Values sent between devices are 32-bit elements; how exact they have to be, the bound alone decides.
No kernel may reach another device: no remote copies, remote signals or barrier semaphores. Data moves between devices by JAX's collectives and lax.ppermute only.
A program may use at most 128 MiB of HBM per device.

```python
import jax
import jax.numpy as jnp
from jax import lax

MODES = 120
KL = 4
E_DEV = 1024
F_DEV = 3072
HALO = 512
ELEMS = 65536
FACES = 196608
NNZ = 1440


def plant(array, key, least, largest):
    longest = array.shape.index(max(array.shape))
    spots = []
    for shift in (0, 1):
        where = [jax.random.randint(jax.random.fold_in(key, axis), (), 0, length) for axis, length in enumerate(array.shape)]
        where[longest] = (where[longest] + shift) % array.shape[longest]
        spots.append(tuple(where))
    return array.at[spots[0]].set(least).at[spots[1]].set(largest)


def shard_levels(stream_key, extent, cuts, smallest, high):
    gain, own = 1.0, jax.random.fold_in(stream_key, 6)
    for position, shards_of in cuts:
        draws = jnp.exp(jax.random.uniform(jax.random.fold_in(own, position), (shards_of,), jnp.float32, smallest / len(cuts), high / len(cuts)))
        gain = gain * jnp.repeat(draws, extent[position] // shards_of).reshape([-1 if axis == position else 1 for axis in range(len(extent))])
    return gain


def gaussian(own_key, extent, spread, most, split=(), kind=jnp.bfloat16):
    array = spread * jax.random.normal(own_key, extent, jnp.float32)
    if split:
        array = array * shard_levels(own_key, extent, split, -0.22, 0.18)
    return jnp.clip(array, -most, most).astype(kind)


def setup_inputs(seed: int = 0) -> dict:
    seeds = jax.random.split(jax.random.key(seed), 7)
    return {
        "traces": gaussian(seeds[0], (MODES, FACES), 1.0, 6.0, ((0, 4), (1, 64)), jnp.float32),
        "elem_mats": gaussian(seeds[1], (KL + 1, 36, ELEMS), 0.3, 1.8, ((2, 64),), jnp.float32),
        "face_links": plant(jax.random.randint(seeds[2], (6, ELEMS), 0, F_DEV + 2 * HALO), jax.random.fold_in(seeds[2], 1), 0, (F_DEV + 2 * HALO) - 1).astype(jnp.int32),
        "pair_modes": plant(jax.random.randint(seeds[3], (2, NNZ), 0, MODES), jax.random.fold_in(seeds[3], 1), 0, MODES - 1).astype(jnp.int32),
        "pair_terms": plant(jax.random.randint(seeds[4], (NNZ,), 0, KL), jax.random.fold_in(seeds[4], 1), 0, KL - 1).astype(jnp.int32),
        "pair_values": gaussian(seeds[5], (NNZ,), 0.5, 3.0, (), jnp.float32),
    }


def coupling_table(pair_modes, pair_terms, pair_values, mode_count, term_count):
    coupling = jnp.zeros((term_count + 1, mode_count, mode_count), jnp.float32)
    coupling = coupling.at[pair_terms + 1, pair_modes[0], pair_modes[1]].add(pair_values)
    return coupling.at[0].set(jnp.eye(mode_count, dtype=jnp.float32))


def element_terms(values, links, mats):
    gathered = values[:, links]
    square_mats = mats.reshape(mats.shape[0], 6, 6, mats.shape[-1])
    running = square_mats[:, None, :, 0, :] * gathered[None, :, 0, None, :]
    for column in range(1, 6):
        running = running + square_mats[:, None, :, column, :] * gathered[None, :, column, None, :]
    return running


def assemble(local_terms, links, ext_width):
    flat = local_terms.reshape(local_terms.shape[:-2] + (-1,))
    zeros = jnp.zeros(local_terms.shape[:-2] + (ext_width,), jnp.float32)
    return zeros.at[..., links.reshape(-1)].add(flat)


def reference(traces, elem_mats, face_links, pair_modes, pair_terms, pair_values):
    mode_count = traces.shape[0]
    term_count = elem_mats.shape[0] - 1
    coupling = coupling_table(pair_modes, pair_terms, pair_values, mode_count, term_count)
    padded = jnp.pad(traces, ((0, 0), (HALO, HALO)))
    owner_index = (jnp.arange(ELEMS, dtype=jnp.int32) // E_DEV).astype(jnp.int32)
    global_links = (face_links + (owner_index * F_DEV)[None, :]).astype(jnp.int32)
    ext_width = padded.shape[1]
    result = jnp.zeros(traces.shape, jnp.float32)
    for kl_term in range(term_count + 1):
        local_terms = element_terms(padded, global_links, elem_mats[kl_term:kl_term + 1])[0]
        assembled = assemble(local_terms, global_links, ext_width)[:, HALO:HALO + FACES]
        result = result + jnp.dot(coupling[kl_term], assembled, precision=lax.Precision.HIGHEST)
    return result
```

```python
import jax
import jax.numpy as jnp
from jax import lax
from jax.experimental import pallas as pl
from jax.experimental.pallas import tpu as pltpu
from jax.sharding import PartitionSpec as P

HALO = 512
MD = 30
SLOTS = 6
E = 1024
OWN = 3072
TERMS = 4
LANES = SLOTS * E
NN = (((1,), (0,)), ((), ()))
NT = (((1,), (1,)), ((), ()))
F32 = jnp.float32
BF16 = jnp.bfloat16


def split_hi_lo(x):
    hi = x.astype(BF16)
    lo = (x - hi.astype(F32)).astype(BF16)
    return hi, lo


def codes(links):
    f = jnp.where(links < HALO, links + OWN, jnp.where(links < HALO + OWN, links - HALO, links))
    quad = (f >> 8) & 3
    row = ((f >> 10) << 8) | (f & 255)
    return row, quad


def table_kernel(me_ref, modes_ref, terms_ref, values_ref, out_ref):
    me = me_ref[0]
    n = values_ref.shape[1]
    i_loc = modes_ref[0:1, :] - MD * me
    row = jnp.where((i_loc >= 0) & (i_loc < MD), terms_ref[...] * 32 + i_loc, -1)
    j = modes_ref[1:2, :]
    part = (j >= MD).astype(jnp.int32) + (j >= 2 * MD).astype(jnp.int32) + (j >= 3 * MD).astype(jnp.int32)
    col = (part ^ me) * 64 + (j - MD * part)
    rid = lax.broadcasted_iota(jnp.int32, (128, n), 0)
    cid = lax.broadcasted_iota(jnp.int32, (256, n), 0)
    cols = jnp.where((cid & ~32) == col, 1.0, 0.0).astype(BF16)
    left = jnp.where(rid == row, values_ref[...], 0.0)
    a = left.astype(BF16)
    rest = left - a.astype(F32)
    b = rest.astype(BF16)
    c = (rest - b.astype(F32)).astype(BF16)
    total = lax.dot_general(a, cols, NT, preferred_element_type=F32)
    total = total + lax.dot_general(b, cols, NT, preferred_element_type=F32)
    total = total + lax.dot_general(c, cols, NT, preferred_element_type=F32)
    hi, lo = split_hi_lo(total)
    out_ref[0:128, :] = hi
    out_ref[128:256, :] = lo


def coupling_table(me, pair_modes, pair_terms, pair_values):
    n = pair_values.shape[0]
    wide = -(-n // 128) * 128
    modes = jnp.pad(pair_modes, ((0, 0), (0, wide - n)))
    terms = jnp.pad(pair_terms, (0, wide - n)).reshape(1, wide)
    values = jnp.pad(pair_values, (0, wide - n)).reshape(1, wide)
    return pl.pallas_call(
        table_kernel,
        out_shape=jax.ShapeDtypeStruct((256, 256), BF16),
        in_specs=[pl.BlockSpec(memory_space=pltpu.SMEM)] + [pl.BlockSpec(memory_space=pltpu.VMEM)] * 3,
        out_specs=pl.BlockSpec(memory_space=pltpu.VMEM),
    )(me, modes, terms, values)


def gather_kernel(x_ref, h_ref, links_ref, out_ref, t_ref):
    t_ref[...] = jnp.zeros(t_ref.shape, BF16)
    for chunk in range(4):
        for q in range(4):
            if chunk < 3:
                piece = x_ref[:, chunk * 1024 + q * 256 : chunk * 1024 + (q + 1) * 256]
            else:
                piece = h_ref[:, q * 256 : (q + 1) * 256]
            hi, lo = split_hi_lo(piece)
            t_ref[q * 64 : q * 64 + MD, chunk * 256 : (chunk + 1) * 256] = hi
            t_ref[q * 64 + 32 : q * 64 + 32 + MD, chunk * 256 : (chunk + 1) * 256] = lo
    t = t_ref[...]
    step = 512

    def one(i, carry):
        base = pl.multiple_of(i * step, step)
        row, quad = codes(links_ref[:, pl.ds(base, step)])
        rid = lax.broadcasted_iota(jnp.int32, (1024, step), 0)
        hot = jnp.where(rid == row, 1.0, 0.0).astype(BF16)
        got = lax.dot_general(t, hot, NN, preferred_element_type=F32)
        total = jnp.zeros((64, step), F32)
        for q in range(4):
            total = total + jnp.where(quad == q, got[q * 64 : (q + 1) * 64], 0.0)
        out_ref[:, pl.ds(base, step)] = total.astype(BF16)
        return carry

    lax.fori_loop(0, LANES // step, one, 0)


def gather(x, h, links):
    return pl.pallas_call(
        gather_kernel,
        out_shape=jax.ShapeDtypeStruct((64, LANES), BF16),
        in_specs=[pl.BlockSpec(memory_space=pltpu.VMEM)] * 3,
        out_specs=pl.BlockSpec(memory_space=pltpu.VMEM),
        scratch_shapes=[pltpu.VMEM((256, 1024), BF16)],
    )(x, h, links)


def scatter_chunk(l_ref, links_ref, chunk):
    total = jnp.zeros((256, 256), F32)
    for a in range(SLOTS):
        row, _ = codes(links_ref[:, a * E : (a + 1) * E])
        rid = lax.broadcasted_iota(jnp.int32, (256, E), 0) + chunk * 256
        hot = jnp.where(rid == row, 1.0, 0.0).astype(BF16)
        total = total + lax.dot_general(l_ref[:, a * E : (a + 1) * E], hot, NT, preferred_element_type=F32)
    return total


def element_kernel(g0, g1, g2, g3, table_ref, mats_ref, links_ref, l_ref, rims_ref, y_ref):
    step = 256

    def one(i, carry):
        base = pl.multiple_of(i * step, step)
        for b in range(SLOTS):
            here = pl.ds(b * E + base, step)
            right = jnp.concatenate([g[:, here] for g in (g0, g1, g2, g3)], axis=0)
            got = lax.dot_general(table_ref[...], right, NN, preferred_element_type=F32)
            own = g0[:, here].astype(F32)
            y_ref[b, 0:32] = own[0:32] + own[32:64]
            y_ref[b, 32:160] = got[0:128] + got[128:256]
        for a in range(SLOTS):
            acc = None
            for b in range(SLOTS):
                for k in range(TERMS + 1):
                    m = mats_ref[k, 6 * a + b : 6 * a + b + 1, pl.ds(base, step)]
                    term = m * y_ref[b, 32 * k : 32 * (k + 1)]
                    acc = term if acc is None else acc + term
            here = pl.ds(a * E + base, step)
            _, quad = codes(links_ref[:, here])
            hi = acc.astype(BF16).astype(F32)
            lo = acc - hi
            for q in range(4):
                l_ref[q * 64 : q * 64 + 32, here] = jnp.where(quad == q, hi, 0.0).astype(BF16)
                l_ref[q * 64 + 32 : q * 64 + 64, here] = jnp.where(quad == q, lo, 0.0).astype(BF16)
        return carry

    lax.fori_loop(0, E // step, one, 0)
    total = scatter_chunk(l_ref, links_ref, 3)
    for q in range(4):
        both = total[q * 64 : q * 64 + 32] + total[q * 64 + 32 : q * 64 + 64]
        rims_ref[:, q * 256 : (q + 1) * 256] = both[0:MD]


def elements(gs, table, mats, links):
    return pl.pallas_call(
        element_kernel,
        out_shape=(jax.ShapeDtypeStruct((256, LANES), BF16), jax.ShapeDtypeStruct((MD, 2 * HALO), F32)),
        in_specs=[pl.BlockSpec(memory_space=pltpu.VMEM)] * 7,
        out_specs=(pl.BlockSpec(memory_space=pltpu.VMEM),) * 2,
        scratch_shapes=[pltpu.VMEM((SLOTS, 160, 256), F32)],
    )(*gs, table, mats, links)


def own_kernel(l_ref, links_ref, out_ref):
    for chunk in range(3):
        total = scatter_chunk(l_ref, links_ref, chunk)
        for q in range(4):
            both = total[q * 64 : q * 64 + 32] + total[q * 64 + 32 : q * 64 + 64]
            out_ref[:, chunk * 1024 + q * 256 : chunk * 1024 + (q + 1) * 256] = both[0:MD]


def scatter_own(l, links):
    return pl.pallas_call(
        own_kernel,
        out_shape=jax.ShapeDtypeStruct((MD, OWN), F32),
        in_specs=[pl.BlockSpec(memory_space=pltpu.VMEM)] * 2,
        out_specs=pl.BlockSpec(memory_space=pltpu.VMEM),
    )(l, links)


def body(traces, elem_mats, face_links, pair_modes, pair_terms, pair_values):
    parts = lax.axis_size("space")
    me = lax.axis_index("mode").astype(jnp.int32).reshape(1)
    up = [(i, i + 1) for i in range(parts - 1)]
    down = [(i + 1, i) for i in range(parts - 1)]
    xor = lambda d: [(i, i ^ d) for i in range(4)]
    others = {d: lax.ppermute(traces, "mode", xor(d)) for d in (2, 1, 3)}
    left = lax.ppermute(traces[:, OWN - HALO :], "space", up)
    right = lax.ppermute(traces[:, :HALO], "space", down)
    halo = jnp.concatenate([left, right], axis=1)
    halos = {d: lax.ppermute(halo, "mode", xor(d)) for d in (2, 1, 3)}
    links = face_links.reshape(1, LANES)
    table = coupling_table(me, pair_modes, pair_terms, pair_values)
    gs = [gather(traces, halo, links)] + [gather(others[d], halos[d], links) for d in (1, 2, 3)]
    local, rims = elements(gs, table, elem_mats, links)
    own = scatter_own(local, links)
    from_next = lax.ppermute(rims[:, :HALO], "space", down)
    from_prev = lax.ppermute(rims[:, HALO:], "space", up)
    return jnp.concatenate(
        [own[:, :HALO] + from_prev, own[:, HALO : OWN - HALO], own[:, OWN - HALO :] + from_next], axis=1
    )


def solution(mesh):
    return jax.shard_map(
        body,
        mesh=mesh,
        in_specs=(P("mode", "space"), P(None, None, "space"), P(None, "space"), P(), P(), P()),
        out_specs=P("mode", "space"),
        check_vma=False,
    )
```

```python
import jax
import jax.numpy as jnp
from jax import lax
from jax.experimental import pallas as pl
from jax.experimental.pallas import tpu as pltpu
from jax.sharding import PartitionSpec as P


HALO = 512
MD = 30
SLOTS = 6
E = 1024
OWN = 3072
TERMS = 4
LANES = SLOTS * E
NN = (((1,), (0,)), ((), ()))
NT = (((1,), (1,)), ((), ()))
F32 = jnp.float32
BF16 = jnp.bfloat16
STEP = 512
VMEM = pl.BlockSpec(memory_space=pltpu.VMEM)
PARAMS = pltpu.CompilerParams(vmem_limit_bytes=16 << 20)


def split_hi_lo(x):
    hi = x.astype(BF16)
    lo = (x - hi.astype(F32)).astype(BF16)
    return hi, lo


def remap(links, odd):
    own = links - HALO
    mine = jnp.where(own < HALO, own, jnp.where(own < OWN - HALO, own + HALO, own - (OWN - 2 * HALO)))
    left = links + OWN + HALO * odd
    right = links - HALO * odd
    return jnp.where(links < HALO, left, jnp.where(links < HALO + OWN, mine, right))


def codes(faces):
    return faces >> 10, (faces >> 8) & 3, faces & 255


def one_hot(chunk_of, row, chunk):
    n = row.shape[1]
    ids = lax.broadcasted_iota(jnp.int32, (256, n), 0).astype(F32).astype(BF16)
    mine = jnp.where(chunk_of == chunk, row, -1).astype(F32).astype(BF16)
    return jnp.where(ids == mine, jnp.ones((), BF16), jnp.zeros((), BF16))


def fill(piece, t_ref, base, lane):
    n = piece.shape[0]
    hi, lo = split_hi_lo(piece)
    t_ref[base : base + n, lane : lane + 256] = hi
    t_ref[base + 32 : base + 32 + n, lane : lane + 256] = lo


def pick(got, quad):
    total = jnp.zeros((64, got.shape[1]), F32)
    for q in range(4):
        total = total + jnp.where(quad == q, got[q * 64 : (q + 1) * 64], 0.0)
    return total.astype(BF16)


def table_kernel(me_ref, modes_ref, terms_ref, values_ref, out_ref):
    me = me_ref[0]
    n = values_ref.shape[1]
    i_loc = modes_ref[0:1, :] - MD * me
    row = jnp.where((i_loc >= 0) & (i_loc < MD), terms_ref[...] * 32 + i_loc, -1)
    j = modes_ref[1:2, :]
    part = (j >= MD).astype(jnp.int32) + (j >= 2 * MD).astype(jnp.int32) + (j >= 3 * MD).astype(jnp.int32)
    col = (part ^ me) * 64 + (j - MD * part)
    rid = lax.broadcasted_iota(jnp.int32, (128, n), 0)
    cid = lax.broadcasted_iota(jnp.int32, (256, n), 0)
    cols = jnp.where((cid & ~32) == col, 1.0, 0.0).astype(BF16)
    left = jnp.where(rid == row, values_ref[...], 0.0)
    a = left.astype(BF16)
    rest = left - a.astype(F32)
    b = rest.astype(BF16)
    c = (rest - b.astype(F32)).astype(BF16)
    total = lax.dot_general(a, cols, NT, preferred_element_type=F32)
    total = total + lax.dot_general(b, cols, NT, preferred_element_type=F32)
    total = total + lax.dot_general(c, cols, NT, preferred_element_type=F32)
    hi, lo = split_hi_lo(total)
    out_ref[0:128, :] = hi
    out_ref[128:256, :] = lo


def coupling_table(me, pair_modes, pair_terms, pair_values):
    n = pair_values.shape[0]
    wide = -(-n // 128) * 128
    modes = jnp.pad(pair_modes, ((0, 0), (0, wide - n)))
    terms = jnp.pad(pair_terms, (0, wide - n)).reshape(1, wide)
    values = jnp.pad(pair_values, (0, wide - n)).reshape(1, wide)
    return pl.pallas_call(
        table_kernel,
        out_shape=jax.ShapeDtypeStruct((256, 256), BF16),
        in_specs=[pl.BlockSpec(memory_space=pltpu.SMEM)] + [VMEM] * 3,
        out_specs=VMEM,
        compiler_params=PARAMS,
    )(me, modes, terms, values)


def gather_body(piece, links_ref, out_ref, t_ref):
    for r in range(8):
        t_ref[r * 32 + 16 : r * 32 + 32, :] = jnp.zeros((16, 768), BF16)
    for c in range(3):
        for q in range(4):
            fill(piece(c, q), t_ref, q * 64, c * 256)
    for b in range(SLOTS):
        chunk_of, quad, row = codes(links_ref[b : b + 1, :])
        hot = jnp.concatenate([one_hot(chunk_of, row, c) for c in range(3)], axis=0)
        got = lax.dot_general(t_ref[...], hot, NN, preferred_element_type=F32)
        out_ref[:, b * E : (b + 1) * E] = pick(got, jnp.where(chunk_of < 3, quad, -1))


def gather_whole_kernel(x_ref, links_ref, out_ref, t_ref):
    def piece(c, q):
        first = HALO + (c - 1) * 1024 + q * 256 if c else q * 256 + (q // 2) * (OWN - 2 * HALO)
        return x_ref[:, first : first + 256]

    gather_body(piece, links_ref, out_ref, t_ref)


def gather_parts_kernel(rims_ref, inside_ref, links_ref, out_ref, t_ref):
    def piece(c, q):
        first = (c - 1) * 1024 + q * 256
        return inside_ref[:, first : first + 256] if c else rims_ref[:, q * 256 : (q + 1) * 256]

    gather_body(piece, links_ref, out_ref, t_ref)


def gather_own(links, *xs):
    return pl.pallas_call(
        gather_whole_kernel if len(xs) == 1 else gather_parts_kernel,
        out_shape=jax.ShapeDtypeStruct((64, LANES), BF16),
        in_specs=[VMEM] * (len(xs) + 1),
        out_specs=VMEM,
        scratch_shapes=[pltpu.VMEM((256, 768), BF16)],
        compiler_params=PARAMS,
    )(*xs, links)


def gather_halo_kernel(o0, o2, o13, inner, links_ref, out_ref, t_ref):
    for r in range(32):
        t_ref[r * 32 + 16 : r * 32 + 32, :] = jnp.zeros((16, 256), BF16)
    for d, (o, first) in enumerate(((o0, 0), (o13, 0), (o2, 0), (o13, MD))):
        for q in range(2):
            fill(o[first : first + MD, q * 256 : (q + 1) * 256], t_ref, (d * 4 + q) * 64, 0)
            fill(inner[d * MD : (d + 1) * MD, q * 256 : (q + 1) * 256], t_ref, (d * 4 + 2 + q) * 64, 0)
    for b in range(SLOTS):
        chunk_of, quad, row = codes(links_ref[b : b + 1, :])
        hot = one_hot(chunk_of, row, 3)
        for d in range(4):
            got = lax.dot_general(t_ref[d * 256 : (d + 1) * 256, :], hot, NN, preferred_element_type=F32)
            out_ref[d * 64 : (d + 1) * 64, b * E : (b + 1) * E] = pick(got, quad)


def gather_halo(o0, o2, o13, inner, links):
    return pl.pallas_call(
        gather_halo_kernel,
        out_shape=jax.ShapeDtypeStruct((256, LANES), BF16),
        in_specs=[VMEM] * 5,
        out_specs=VMEM,
        scratch_shapes=[pltpu.VMEM((1024, 256), BF16)],
        compiler_params=PARAMS,
    )(o0, o2, o13, inner, links)


def scatter_chunk(l_ref, links_ref, chunk):
    total = None
    for a in range(SLOTS):
        chunk_of, _, row = codes(links_ref[a : a + 1, :])
        hot = one_hot(chunk_of, row, chunk)
        part = lax.dot_general(l_ref[:, a * E : (a + 1) * E], hot, NT, preferred_element_type=F32)
        total = part if total is None else total + part
    return total


def element_kernel(g0, g1, g2, g3, gh, table_ref, mats_ref, links_ref, l_ref, rims_ref, y_ref):
    def one(i, carry):
        base = pl.multiple_of(i * STEP, STEP)
        for b in range(SLOTS):
            here = pl.ds(b * E + base, STEP)
            right = jnp.concatenate([g[:, here] for g in (g0, g1, g2, g3)], axis=0) + gh[:, here]
            got = lax.dot_general(table_ref[...], right, NN, preferred_element_type=F32)
            own = right[0:64].astype(F32)
            y_ref[b, 0:32] = own[0:32] + own[32:64]
            y_ref[b, 32:160] = got[0:128] + got[128:256]
        for a in range(SLOTS):
            acc = None
            for b in range(SLOTS):
                for k in range(TERMS + 1):
                    m = mats_ref[k, 6 * a + b : 6 * a + b + 1, pl.ds(base, STEP)]
                    term = m * y_ref[b, 32 * k : 32 * (k + 1)]
                    acc = term if acc is None else acc + term
            here = pl.ds(a * E + base, STEP)
            _, quad, _ = codes(links_ref[a : a + 1, pl.ds(base, STEP)])
            hi = acc.astype(BF16).astype(F32)
            lo = acc - hi
            for q in range(4):
                l_ref[q * 64 : q * 64 + 32, here] = jnp.where(quad == q, hi, 0.0).astype(BF16)
                l_ref[q * 64 + 32 : q * 64 + 64, here] = jnp.where(quad == q, lo, 0.0).astype(BF16)
        return carry

    lax.fori_loop(0, E // STEP, one, 0)
    total = scatter_chunk(l_ref, links_ref, 3)
    for q in range(4):
        both = total[q * 64 : q * 64 + 32] + total[q * 64 + 32 : q * 64 + 64]
        rims_ref[:, q * 256 : (q + 1) * 256] = both[0:MD]


def elements(gs, halo, table, mats, links):
    return pl.pallas_call(
        element_kernel,
        out_shape=(jax.ShapeDtypeStruct((256, LANES), BF16), jax.ShapeDtypeStruct((MD, 2 * HALO), F32)),
        in_specs=[VMEM] * 8,
        out_specs=(VMEM, VMEM),
        scratch_shapes=[pltpu.VMEM((SLOTS, 160, STEP), F32)],
        compiler_params=PARAMS,
    )(*gs, halo, table, mats, links)


def own_kernel(l_ref, links_ref, out_ref):
    for chunk in range(3):
        total = scatter_chunk(l_ref, links_ref, chunk)
        for q in range(4):
            both = total[q * 64 : q * 64 + 32] + total[q * 64 + 32 : q * 64 + 64]
            first = HALO + (chunk - 1) * 1024 + q * 256 if chunk else q * 256 + (q // 2) * (OWN - 2 * HALO)
            out_ref[:, first : first + 256] = both[0:MD]


def scatter_own(l, links):
    return pl.pallas_call(
        own_kernel,
        out_shape=jax.ShapeDtypeStruct((MD, OWN), F32),
        in_specs=[VMEM] * 2,
        out_specs=VMEM,
        compiler_params=PARAMS,
    )(l, links)


def finish_kernel(odd_ref, own_ref, out_in_ref, in_in_ref, out_ref):
    odd = odd_ref[0] == 1
    outer = out_in_ref[...]
    inner = in_in_ref[...]
    out_ref[:, HALO : OWN - HALO] = own_ref[:, HALO : OWN - HALO]
    out_ref[:, :HALO] = own_ref[:, :HALO] + jnp.where(odd, inner, outer)
    out_ref[:, OWN - HALO :] = own_ref[:, OWN - HALO :] + jnp.where(odd, outer, inner)


def finish(odd, own, outer, inner):
    return pl.pallas_call(
        finish_kernel,
        out_shape=jax.ShapeDtypeStruct((MD, OWN), F32),
        in_specs=[pl.BlockSpec(memory_space=pltpu.SMEM)] + [VMEM] * 3,
        out_specs=VMEM,
        compiler_params=PARAMS,
    )(odd, own, outer, inner)


def body(traces, elem_mats, face_links, pair_modes, pair_terms, pair_values):
    parts = lax.axis_size("space")
    me = lax.axis_index("mode").astype(jnp.int32).reshape(1)
    odd = lax.axis_index("space").astype(jnp.int32) % 2
    outer_pairs = [(i, i + 1) for i in range(1, parts - 1, 2)] + [(i + 1, i) for i in range(1, parts - 1, 2)]
    inner_pairs = [(i, i ^ 1) for i in range(parts)]
    near = [(i, i ^ 1) for i in range(4)]
    far = [(i, i ^ 2) for i in range(4)]
    links = remap(face_links, odd)
    rims = jnp.concatenate([traces[:, :HALO], traces[:, OWN - HALO :]], axis=1)
    x2a = lax.ppermute(rims, "mode", far)
    x1 = lax.ppermute(traces, "mode", near)
    o0 = lax.ppermute(lax.dynamic_slice_in_dim(rims, HALO * odd, HALO, axis=1), "space", outer_pairs)
    x2b = lax.ppermute(traces[:, HALO : OWN - HALO], "mode", far)
    x3a = lax.ppermute(x2a, "mode", near)
    o2 = lax.ppermute(o0, "mode", far)
    x3b = lax.ppermute(x2b, "mode", near)
    o13 = lax.ppermute(jnp.concatenate([o0, o2], axis=0), "mode", near)
    near_rims = jnp.concatenate([x1[:, :HALO], x1[:, OWN - HALO :]], axis=1)
    all_rims = jnp.concatenate([rims, near_rims, x2a, x3a], axis=0)
    inner = lax.ppermute(lax.dynamic_slice_in_dim(all_rims, HALO * (1 - odd), HALO, axis=1), "space", inner_pairs)
    table = coupling_table(me, pair_modes, pair_terms, pair_values)
    g0 = gather_own(links, traces)
    g1 = gather_own(links, x1)
    g2 = gather_own(links, x2a, x2b)
    g3 = gather_own(links, x3a, x3b)
    halo = gather_halo(o0, o2, o13, inner, links)
    local, back = elements((g0, g1, g2, g3), halo, table, elem_mats, links)
    back_outer = lax.ppermute(back[:, :HALO], "space", outer_pairs)
    back_inner = lax.ppermute(back[:, HALO:], "space", inner_pairs)
    own = scatter_own(local, links)
    return finish(odd.reshape(1), own, back_outer, back_inner)


def solution(mesh):
    return jax.shard_map(
        body,
        mesh=mesh,
        in_specs=(P("mode", "space"), P(None, None, "space"), P(None, "space"), P(), P(), P()),
        out_specs=P("mode", "space"),
        check_vma=False,
    )
```

```python
import functools

import jax
import jax.numpy as jnp
from jax import lax
from jax.experimental import pallas as pl
from jax.experimental.pallas import tpu as pltpu
from jax.sharding import PartitionSpec as P


HALO = 512
MD = 30
SLOTS = 6
E = 1024
OWN = 3072
TERMS = 4
LANES = SLOTS * E
NN = (((1,), (0,)), ((), ()))
NT = (((1,), (1,)), ((), ()))
F32 = jnp.float32
BF16 = jnp.bfloat16
STEP = 512
VMEM = pl.BlockSpec(memory_space=pltpu.VMEM)
PARAMS = pltpu.CompilerParams(vmem_limit_bytes=16 << 20)


def split_hi_lo(x):
    hi = x.astype(BF16)
    lo = (x - hi.astype(F32)).astype(BF16)
    return hi, lo


def codes(links, odd):
    own = links - HALO
    mine = jnp.where(own < HALO, own, jnp.where(own < OWN - HALO, own + HALO, own - (OWN - 2 * HALO)))
    left = links + OWN + HALO * odd
    right = links - HALO * odd
    faces = jnp.where(links < HALO, left, jnp.where(links < HALO + OWN, mine, right))
    return faces >> 10, (faces >> 8) & 3, faces & 255


def one_hot(chunk_of, row, chunk):
    n = row.shape[1]
    ids = lax.broadcasted_iota(jnp.int32, (256, n), 0).astype(F32).astype(BF16)
    mine = jnp.where(chunk_of == chunk, row, -1).astype(F32).astype(BF16)
    return jnp.where(ids == mine, jnp.ones((), BF16), jnp.zeros((), BF16))


def fill(piece, t_ref, base, lane):
    n = piece.shape[0]
    hi, lo = split_hi_lo(piece)
    t_ref[base : base + n, lane : lane + 256] = hi
    t_ref[base + 32 : base + 32 + n, lane : lane + 256] = lo


def pick(got, quad):
    total = jnp.zeros((64, got.shape[1]), F32)
    for q in range(4):
        total = total + jnp.where(quad == q, got[q * 64 : (q + 1) * 64], 0.0)
    return total.astype(BF16)


def table_kernel(me_ref, modes_ref, terms_ref, values_ref, out_ref, ids_ref, v_ref):
    me = me_ref[0]
    n = values_ref.shape[1]
    wide = v_ref.shape[1]
    ids_ref[...] = jnp.full(ids_ref.shape, -1, jnp.int32)
    v_ref[...] = jnp.zeros(v_ref.shape, F32)
    v_ref[0:1, 0:n] = values_ref[...]
    i_loc = modes_ref[0:1, :] - MD * me
    ids_ref[0:1, 0:n] = jnp.where((i_loc >= 0) & (i_loc < MD), terms_ref[...] * 32 + i_loc, -1)
    j = modes_ref[1:2, :]
    part = (j >= MD).astype(jnp.int32) + (j >= 2 * MD).astype(jnp.int32) + (j >= 3 * MD).astype(jnp.int32)
    ids_ref[1:2, 0:n] = (part ^ me) * 64 + (j - MD * part)
    rid = lax.broadcasted_iota(jnp.int32, (128, wide), 0)
    cid = lax.broadcasted_iota(jnp.int32, (256, wide), 0)
    cols = jnp.where((cid & ~32) == ids_ref[1:2, :], 1.0, 0.0).astype(BF16)
    left = jnp.where(rid == ids_ref[0:1, :], v_ref[0:1, :], 0.0)
    a = left.astype(BF16)
    rest = left - a.astype(F32)
    b = rest.astype(BF16)
    c = (rest - b.astype(F32)).astype(BF16)
    total = lax.dot_general(a, cols, NT, preferred_element_type=F32)
    total = total + lax.dot_general(b, cols, NT, preferred_element_type=F32)
    total = total + lax.dot_general(c, cols, NT, preferred_element_type=F32)
    hi, lo = split_hi_lo(total)
    out_ref[0:128, :] = hi
    out_ref[128:256, :] = lo


SMEM = pl.BlockSpec(memory_space=pltpu.SMEM)


def coupling_table(me, pair_modes, pair_terms, pair_values):
    n = pair_values.shape[0]
    wide = -(-n // 128) * 128
    return pl.pallas_call(
        table_kernel,
        out_shape=jax.ShapeDtypeStruct((256, 256), BF16),
        in_specs=[SMEM] + [VMEM] * 3,
        out_specs=VMEM,
        scratch_shapes=[pltpu.VMEM((8, wide), jnp.int32), pltpu.VMEM((8, wide), F32)],
        compiler_params=PARAMS,
    )(me, pair_modes, pair_terms.reshape(1, n), pair_values.reshape(1, n))


def gather_body(piece, odd_ref, links_ref, out_ref, t_ref):
    for r in range(8):
        t_ref[r * 32 + 16 : r * 32 + 32, :] = jnp.zeros((16, 768), BF16)
    for c in range(3):
        for q in range(4):
            fill(piece(c, q), t_ref, q * 64, c * 256)
    for b in range(SLOTS):
        chunk_of, quad, row = codes(links_ref[b : b + 1, :], odd_ref[0])
        hot = jnp.concatenate([one_hot(chunk_of, row, c) for c in range(3)], axis=0)
        got = lax.dot_general(t_ref[...], hot, NN, preferred_element_type=F32)
        out_ref[:, b * E : (b + 1) * E] = pick(got, jnp.where(chunk_of < 3, quad, -1))


def gather_whole_kernel(odd_ref, x_ref, links_ref, out_ref, t_ref):
    def piece(c, q):
        first = HALO + (c - 1) * 1024 + q * 256 if c else q * 256 + (q // 2) * (OWN - 2 * HALO)
        return x_ref[:, first : first + 256]

    gather_body(piece, odd_ref, links_ref, out_ref, t_ref)


def gather_parts_kernel(odd_ref, rims_ref, inside_ref, links_ref, out_ref, t_ref):
    def piece(c, q):
        first = (c - 1) * 1024 + q * 256
        return inside_ref[:, first : first + 256] if c else rims_ref[:, q * 256 : (q + 1) * 256]

    gather_body(piece, odd_ref, links_ref, out_ref, t_ref)


def gather_own(odd, links, *xs):
    return pl.pallas_call(
        gather_whole_kernel if len(xs) == 1 else gather_parts_kernel,
        out_shape=jax.ShapeDtypeStruct((64, LANES), BF16),
        in_specs=[SMEM] + [VMEM] * (len(xs) + 1),
        out_specs=VMEM,
        scratch_shapes=[pltpu.VMEM((256, 768), BF16)],
        compiler_params=PARAMS,
    )(odd, *xs, links)


def gather_halo_kernel(half, odd_ref, outer_ref, inner_ref, links_ref, out_ref, t_ref):
    for r in range(16):
        t_ref[r * 32 + 16 : r * 32 + 32, :] = jnp.zeros((16, 256), BF16)
    for d in range(2):
        for q in range(2):
            here = slice(q * 256, (q + 1) * 256)
            fill(outer_ref[d * MD : (d + 1) * MD, here], t_ref, (d * 4 + q) * 64, 0)
            first = (2 * half + d) * MD
            fill(inner_ref[first : first + MD, here], t_ref, (d * 4 + 2 + q) * 64, 0)
    for b in range(SLOTS):
        chunk_of, quad, row = codes(links_ref[b : b + 1, :], odd_ref[0])
        hot = one_hot(chunk_of, row, 3)
        for d in range(2):
            got = lax.dot_general(t_ref[d * 256 : (d + 1) * 256, :], hot, NN, preferred_element_type=F32)
            out_ref[d * 64 : (d + 1) * 64, b * E : (b + 1) * E] = pick(got, quad)


def gather_halo(odd, links, outer, inner, half):
    return pl.pallas_call(
        functools.partial(gather_halo_kernel, half),
        out_shape=jax.ShapeDtypeStruct((128, LANES), BF16),
        in_specs=[SMEM] + [VMEM] * 3,
        out_specs=VMEM,
        scratch_shapes=[pltpu.VMEM((512, 256), BF16)],
        compiler_params=PARAMS,
    )(odd, outer, inner, links)


def scatter_chunk(odd_ref, l_ref, links_ref, chunk):
    total = None
    for a in range(SLOTS):
        chunk_of, _, row = codes(links_ref[a : a + 1, :], odd_ref[0])
        hot = one_hot(chunk_of, row, chunk)
        part = lax.dot_general(l_ref[:, a * E : (a + 1) * E], hot, NT, preferred_element_type=F32)
        total = part if total is None else total + part
    return total


def element_kernel(odd_ref, g0, g1, g2, g3, ha, hb, table_ref, mats_ref, links_ref, l_ref, outer_ref, inner_ref, y_ref):
    def one(i, carry):
        base = pl.multiple_of(i * STEP, STEP)
        for b in range(SLOTS):
            here = pl.ds(b * E + base, STEP)
            right = jnp.concatenate(
                [
                    g0[:, here] + ha[0:64, here],
                    g1[:, here] + hb[0:64, here],
                    g2[:, here] + ha[64:128, here],
                    g3[:, here] + hb[64:128, here],
                ],
                axis=0,
            )
            got = lax.dot_general(table_ref[...], right, NN, preferred_element_type=F32)
            own = right[0:64].astype(F32)
            y_ref[b, 0:32] = own[0:32] + own[32:64]
            y_ref[b, 32:160] = got[0:128] + got[128:256]
        for a in range(SLOTS):
            acc = None
            for b in range(SLOTS):
                for k in range(TERMS + 1):
                    m = mats_ref[k, 6 * a + b : 6 * a + b + 1, pl.ds(base, STEP)]
                    term = m * y_ref[b, 32 * k : 32 * (k + 1)]
                    acc = term if acc is None else acc + term
            here = pl.ds(a * E + base, STEP)
            _, quad, _ = codes(links_ref[a : a + 1, pl.ds(base, STEP)], odd_ref[0])
            hi = acc.astype(BF16).astype(F32)
            lo = acc - hi
            for q in range(4):
                l_ref[q * 64 : q * 64 + 32, here] = jnp.where(quad == q, hi, 0.0).astype(BF16)
                l_ref[q * 64 + 32 : q * 64 + 64, here] = jnp.where(quad == q, lo, 0.0).astype(BF16)
        return carry

    lax.fori_loop(0, E // STEP, one, 0)
    total = scatter_chunk(odd_ref, l_ref, links_ref, 3)
    for q in range(4):
        both = total[q * 64 : q * 64 + 32] + total[q * 64 + 32 : q * 64 + 64]
        ref = inner_ref if q // 2 else outer_ref
        ref[:, (q % 2) * 256 : (q % 2 + 1) * 256] = both[0:MD]


def elements(odd, gs, halos, table, mats, links):
    rim = jax.ShapeDtypeStruct((MD, HALO), F32)
    return pl.pallas_call(
        element_kernel,
        out_shape=(jax.ShapeDtypeStruct((256, LANES), BF16), rim, rim),
        in_specs=[SMEM] + [VMEM] * 9,
        out_specs=(VMEM, VMEM, VMEM),
        scratch_shapes=[pltpu.VMEM((SLOTS, 160, STEP), F32)],
        compiler_params=PARAMS,
    )(odd, *gs, *halos, table, mats, links)


def own_kernel(odd_ref, l_ref, links_ref, out_ref):
    for chunk in range(3):
        total = scatter_chunk(odd_ref, l_ref, links_ref, chunk)
        for q in range(4):
            both = total[q * 64 : q * 64 + 32] + total[q * 64 + 32 : q * 64 + 64]
            first = HALO + (chunk - 1) * 1024 + q * 256 if chunk else q * 256 + (q // 2) * (OWN - 2 * HALO)
            out_ref[:, first : first + 256] = both[0:MD]


def scatter_own(odd, l, links):
    return pl.pallas_call(
        own_kernel,
        out_shape=jax.ShapeDtypeStruct((MD, OWN), F32),
        in_specs=[SMEM] + [VMEM] * 2,
        out_specs=VMEM,
        compiler_params=PARAMS,
    )(odd, l, links)


def finish_kernel(odd_ref, own_ref, out_in_ref, in_in_ref, out_ref):
    odd = odd_ref[0] == 1
    outer = out_in_ref[...]
    inner = in_in_ref[...]
    out_ref[:, HALO : OWN - HALO] = own_ref[:, HALO : OWN - HALO]
    out_ref[:, :HALO] = own_ref[:, :HALO] + jnp.where(odd, inner, outer)
    out_ref[:, OWN - HALO :] = own_ref[:, OWN - HALO :] + jnp.where(odd, outer, inner)


def finish(odd, own, outer, inner):
    return pl.pallas_call(
        finish_kernel,
        out_shape=jax.ShapeDtypeStruct((MD, OWN), F32),
        in_specs=[pl.BlockSpec(memory_space=pltpu.SMEM)] + [VMEM] * 3,
        out_specs=VMEM,
        compiler_params=PARAMS,
    )(odd, own, outer, inner)


def body(traces, elem_mats, face_links, pair_modes, pair_terms, pair_values):
    parts = lax.axis_size("space")
    me = lax.axis_index("mode").astype(jnp.int32).reshape(1)
    odd = lax.axis_index("space").astype(jnp.int32) % 2
    outer_pairs = [(i, i + 1) for i in range(1, parts - 1, 2)] + [(i + 1, i) for i in range(1, parts - 1, 2)]
    inner_pairs = [(i, i ^ 1) for i in range(parts)]
    near = [(i, i ^ 1) for i in range(4)]
    far = [(i, i ^ 2) for i in range(4)]
    links = face_links
    side = odd.reshape(1)
    rims = jnp.concatenate([traces[:, :HALO], traces[:, OWN - HALO :]], axis=1)
    inside = traces[:, HALO : OWN - HALO]
    x2a = lax.ppermute(rims, "mode", far)
    x1 = lax.ppermute(traces, "mode", near)
    x2b = lax.ppermute(inside, "mode", far)
    g0 = gather_own(side, links, rims, inside)
    to_outer = lax.dynamic_slice_in_dim(jnp.concatenate([rims, x2a], axis=0), HALO * odd, HALO, axis=1)
    to_outer, g0 = lax.optimization_barrier((to_outer, g0))
    o02 = lax.ppermute(to_outer, "space", outer_pairs)
    x3a = lax.ppermute(x2a, "mode", near)
    x3b = lax.ppermute(x2b, "mode", near)
    o13 = lax.ppermute(o02, "mode", near)
    near_rims = jnp.concatenate([x1[:, :HALO], x1[:, OWN - HALO :]], axis=1)
    all_rims = jnp.concatenate([rims, x2a, near_rims, x3a], axis=0)
    inner = lax.ppermute(lax.dynamic_slice_in_dim(all_rims, HALO * (1 - odd), HALO, axis=1), "space", inner_pairs)
    table = coupling_table(me, pair_modes, pair_terms, pair_values)
    g1 = gather_own(side, links, x1)
    g2 = gather_own(side, links, x2a, x2b)
    g3 = gather_own(side, links, x3a, x3b)
    ha = gather_halo(side, links, o02, inner, 0)
    hb = gather_halo(side, links, o13, inner, 1)
    local, to_back, to_sibling = elements(side, (g0, g1, g2, g3), (ha, hb), table, elem_mats, links)
    back_outer = lax.ppermute(to_back, "space", outer_pairs)
    back_inner = lax.ppermute(to_sibling, "space", inner_pairs)
    own = scatter_own(side, local, links)
    return finish(side, own, back_outer, back_inner)


def solution(mesh):
    return jax.shard_map(
        body,
        mesh=mesh,
        in_specs=(P("mode", "space"), P(None, None, "space"), P(None, "space"), P(), P(), P()),
        out_specs=P("mode", "space"),
        check_vma=False,
    )
```

```python
import functools

import jax
import jax.numpy as jnp
from jax import lax
from jax.experimental import pallas as pl
from jax.experimental.pallas import tpu as pltpu
from jax.sharding import PartitionSpec as P


HALO = 512
MD = 30
SLOTS = 6
E = 1024
OWN = 3072
TERMS = 4
LANES = SLOTS * E
NN = (((1,), (0,)), ((), ()))
NT = (((1,), (1,)), ((), ()))
F32 = jnp.float32
BF16 = jnp.bfloat16
STEP = 512
VMEM = pl.BlockSpec(memory_space=pltpu.VMEM)
PARAMS = pltpu.CompilerParams(vmem_limit_bytes=16 << 20)


def split_hi_lo(x):
    hi = x.astype(BF16)
    lo = (x - hi.astype(F32)).astype(BF16)
    return hi, lo


def codes(links, odd):
    own = links - HALO
    mine = jnp.where(own < HALO, own, jnp.where(own < OWN - HALO, own + HALO, own - (OWN - 2 * HALO)))
    left = links + OWN + HALO * odd
    right = links - HALO * odd
    faces = jnp.where(links < HALO, left, jnp.where(links < HALO + OWN, mine, right))
    return faces >> 10, (faces >> 8) & 3, faces & 255


def one_hot(chunk_of, row, chunk):
    n = row.shape[1]
    ids = lax.broadcasted_iota(jnp.int32, (256, n), 0).astype(F32).astype(BF16)
    mine = jnp.where(chunk_of == chunk, row, -1).astype(F32).astype(BF16)
    return jnp.where(ids == mine, jnp.ones((), BF16), jnp.zeros((), BF16))


def fill(piece, t_ref, base, lane):
    n = piece.shape[0]
    hi, lo = split_hi_lo(piece)
    t_ref[base : base + n, lane : lane + 256] = hi
    t_ref[base + 32 : base + 32 + n, lane : lane + 256] = lo


def pick(got, quad):
    total = jnp.zeros((64, got.shape[1]), F32)
    for q in range(4):
        total = total + jnp.where(quad == q, got[q * 64 : (q + 1) * 64], 0.0)
    return total.astype(BF16)


def table_kernel(me_ref, modes_ref, terms_ref, values_ref, out_ref, ids_ref, v_ref):
    me = me_ref[0]
    n = values_ref.shape[0]
    wide = v_ref.shape[1]
    ids_ref[...] = jnp.full(ids_ref.shape, -1, jnp.int32)
    v_ref[...] = jnp.zeros(v_ref.shape, F32)
    v_ref[0, 0:n] = values_ref[...]
    ids_ref[2, 0:n] = terms_ref[...]
    i_loc = modes_ref[0:1, :] - MD * me
    ids_ref[0:1, 0:n] = jnp.where((i_loc >= 0) & (i_loc < MD), ids_ref[2:3, 0:n] * 32 + i_loc, -1)
    j = modes_ref[1:2, :]
    part = (j >= MD).astype(jnp.int32) + (j >= 2 * MD).astype(jnp.int32) + (j >= 3 * MD).astype(jnp.int32)
    ids_ref[1:2, 0:n] = (part ^ me) * 64 + (j - MD * part)
    rid = lax.broadcasted_iota(jnp.int32, (128, wide), 0)
    cid = lax.broadcasted_iota(jnp.int32, (256, wide), 0)
    cols = jnp.where((cid & ~32) == ids_ref[1:2, :], 1.0, 0.0).astype(BF16)
    left = jnp.where(rid == ids_ref[0:1, :], v_ref[0:1, :], 0.0)
    a = left.astype(BF16)
    rest = left - a.astype(F32)
    b = rest.astype(BF16)
    c = (rest - b.astype(F32)).astype(BF16)
    total = lax.dot_general(a, cols, NT, preferred_element_type=F32)
    total = total + lax.dot_general(b, cols, NT, preferred_element_type=F32)
    total = total + lax.dot_general(c, cols, NT, preferred_element_type=F32)
    hi, lo = split_hi_lo(total)
    out_ref[0:128, :] = hi
    out_ref[128:256, :] = lo


SMEM = pl.BlockSpec(memory_space=pltpu.SMEM)


def coupling_table(me, pair_modes, pair_terms, pair_values):
    n = pair_values.shape[0]
    wide = -(-n // 128) * 128
    return pl.pallas_call(
        table_kernel,
        out_shape=jax.ShapeDtypeStruct((256, 256), BF16),
        in_specs=[SMEM] + [VMEM] * 3,
        out_specs=VMEM,
        scratch_shapes=[pltpu.VMEM((8, wide), jnp.int32), pltpu.VMEM((8, wide), F32)],
        compiler_params=PARAMS,
    )(me, pair_modes, pair_terms, pair_values)


def gather_body(piece, odd_ref, links_ref, out_ref, t_ref):
    for r in range(8):
        t_ref[r * 32 + 16 : r * 32 + 32, :] = jnp.zeros((16, 768), BF16)
    for c in range(3):
        for q in range(4):
            fill(piece(c, q), t_ref, q * 64, c * 256)
    for b in range(SLOTS):
        chunk_of, quad, row = codes(links_ref[b : b + 1, :], odd_ref[0])
        hot = jnp.concatenate([one_hot(chunk_of, row, c) for c in range(3)], axis=0)
        got = lax.dot_general(t_ref[...], hot, NN, preferred_element_type=F32)
        out_ref[:, b * E : (b + 1) * E] = pick(got, jnp.where(chunk_of < 3, quad, -1))


def gather_whole_kernel(odd_ref, x_ref, links_ref, out_ref, t_ref):
    def piece(c, q):
        first = HALO + (c - 1) * 1024 + q * 256 if c else q * 256 + (q // 2) * (OWN - 2 * HALO)
        return x_ref[:, first : first + 256]

    gather_body(piece, odd_ref, links_ref, out_ref, t_ref)


def gather_parts_kernel(odd_ref, rims_ref, inside_ref, links_ref, out_ref, t_ref):
    def piece(c, q):
        first = (c - 1) * 1024 + q * 256
        return inside_ref[:, first : first + 256] if c else rims_ref[:, q * 256 : (q + 1) * 256]

    gather_body(piece, odd_ref, links_ref, out_ref, t_ref)


def gather_own(odd, links, *xs):
    return pl.pallas_call(
        gather_whole_kernel if len(xs) == 1 else gather_parts_kernel,
        out_shape=jax.ShapeDtypeStruct((64, LANES), BF16),
        in_specs=[SMEM] + [VMEM] * (len(xs) + 1),
        out_specs=VMEM,
        scratch_shapes=[pltpu.VMEM((256, 768), BF16)],
        compiler_params=PARAMS,
    )(odd, *xs, links)


def gather_halo_kernel(half, odd_ref, outer_ref, inner_ref, links_ref, out_ref, t_ref):
    for r in range(16):
        t_ref[r * 32 + 16 : r * 32 + 32, :] = jnp.zeros((16, 256), BF16)
    for d in range(2):
        for q in range(2):
            here = slice(q * 256, (q + 1) * 256)
            fill(outer_ref[d * MD : (d + 1) * MD, here], t_ref, (d * 4 + q) * 64, 0)
            first = (2 * half + d) * MD
            fill(inner_ref[first : first + MD, here], t_ref, (d * 4 + 2 + q) * 64, 0)
    for b in range(SLOTS):
        chunk_of, quad, row = codes(links_ref[b : b + 1, :], odd_ref[0])
        hot = one_hot(chunk_of, row, 3)
        for d in range(2):
            got = lax.dot_general(t_ref[d * 256 : (d + 1) * 256, :], hot, NN, preferred_element_type=F32)
            out_ref[d * 64 : (d + 1) * 64, b * E : (b + 1) * E] = pick(got, quad)


def gather_halo(odd, links, outer, inner, half):
    return pl.pallas_call(
        functools.partial(gather_halo_kernel, half),
        out_shape=jax.ShapeDtypeStruct((128, LANES), BF16),
        in_specs=[SMEM] + [VMEM] * 3,
        out_specs=VMEM,
        scratch_shapes=[pltpu.VMEM((512, 256), BF16)],
        compiler_params=PARAMS,
    )(odd, outer, inner, links)


def scatter_chunk(odd_ref, l_ref, links_ref, chunk):
    total = None
    for a in range(SLOTS):
        chunk_of, _, row = codes(links_ref[a : a + 1, :], odd_ref[0])
        hot = one_hot(chunk_of, row, chunk)
        part = lax.dot_general(l_ref[:, a * E : (a + 1) * E], hot, NT, preferred_element_type=F32)
        total = part if total is None else total + part
    return total


def element_kernel(odd_ref, g0, g1, g2, g3, ha, hb, table_ref, mats_ref, links_ref, l_ref, outer_ref, inner_ref, y_ref):
    def one(i, carry):
        base = pl.multiple_of(i * STEP, STEP)
        for b in range(SLOTS):
            here = pl.ds(b * E + base, STEP)
            right = jnp.concatenate(
                [
                    g0[:, here] + hb[64:128, here],
                    g1[:, here] + ha[64:128, here],
                    g2[:, here] + hb[0:64, here],
                    g3[:, here] + ha[0:64, here],
                ],
                axis=0,
            )
            got = lax.dot_general(table_ref[...], right, NN, preferred_element_type=F32)
            own = right[0:64].astype(F32)
            y_ref[b, 0:32] = own[0:32] + own[32:64]
            y_ref[b, 32:160] = got[0:128] + got[128:256]
        for a in range(SLOTS):
            acc = None
            for b in range(SLOTS):
                for k in range(TERMS + 1):
                    m = mats_ref[k, 6 * a + b : 6 * a + b + 1, pl.ds(base, STEP)]
                    term = m * y_ref[b, 32 * k : 32 * (k + 1)]
                    acc = term if acc is None else acc + term
            here = pl.ds(a * E + base, STEP)
            _, quad, _ = codes(links_ref[a : a + 1, pl.ds(base, STEP)], odd_ref[0])
            hi = acc.astype(BF16).astype(F32)
            lo = acc - hi
            for q in range(4):
                l_ref[q * 64 : q * 64 + 32, here] = jnp.where(quad == q, hi, 0.0).astype(BF16)
                l_ref[q * 64 + 32 : q * 64 + 64, here] = jnp.where(quad == q, lo, 0.0).astype(BF16)
        return carry

    lax.fori_loop(0, E // STEP, one, 0)
    total = scatter_chunk(odd_ref, l_ref, links_ref, 3)
    for q in range(4):
        both = total[q * 64 : q * 64 + 32] + total[q * 64 + 32 : q * 64 + 64]
        ref = inner_ref if q // 2 else outer_ref
        ref[:, (q % 2) * 256 : (q % 2 + 1) * 256] = both[0:MD]


def elements(odd, gs, halos, table, mats, links):
    rim = jax.ShapeDtypeStruct((MD, HALO), F32)
    return pl.pallas_call(
        element_kernel,
        out_shape=(jax.ShapeDtypeStruct((256, LANES), BF16), rim, rim),
        in_specs=[SMEM] + [VMEM] * 9,
        out_specs=(VMEM, VMEM, VMEM),
        scratch_shapes=[pltpu.VMEM((SLOTS, 160, STEP), F32)],
        compiler_params=PARAMS,
    )(odd, *gs, *halos, table, mats, links)


def own_kernel(odd_ref, l_ref, links_ref, out_ref):
    for chunk in range(3):
        total = scatter_chunk(odd_ref, l_ref, links_ref, chunk)
        for q in range(4):
            both = total[q * 64 : q * 64 + 32] + total[q * 64 + 32 : q * 64 + 64]
            first = HALO + (chunk - 1) * 1024 + q * 256 if chunk else q * 256 + (q // 2) * (OWN - 2 * HALO)
            out_ref[:, first : first + 256] = both[0:MD]


def scatter_own(odd, l, links):
    return pl.pallas_call(
        own_kernel,
        out_shape=jax.ShapeDtypeStruct((MD, OWN), F32),
        in_specs=[SMEM] + [VMEM] * 2,
        out_specs=VMEM,
        compiler_params=PARAMS,
    )(odd, l, links)


def finish_kernel(odd_ref, own_ref, out_in_ref, in_in_ref, out_ref):
    odd = odd_ref[0] == 1
    outer = out_in_ref[...]
    inner = in_in_ref[...]
    out_ref[:, HALO : OWN - HALO] = own_ref[:, HALO : OWN - HALO]
    out_ref[:, :HALO] = own_ref[:, :HALO] + jnp.where(odd, inner, outer)
    out_ref[:, OWN - HALO :] = own_ref[:, OWN - HALO :] + jnp.where(odd, outer, inner)


def finish(odd, own, outer, inner):
    return pl.pallas_call(
        finish_kernel,
        out_shape=jax.ShapeDtypeStruct((MD, OWN), F32),
        in_specs=[pl.BlockSpec(memory_space=pltpu.SMEM)] + [VMEM] * 3,
        out_specs=VMEM,
        compiler_params=PARAMS,
    )(odd, own, outer, inner)


def body(traces, elem_mats, face_links, pair_modes, pair_terms, pair_values):
    parts = lax.axis_size("space")
    me = lax.axis_index("mode").astype(jnp.int32).reshape(1)
    odd = lax.axis_index("space").astype(jnp.int32) % 2
    outer_pairs = [(i, i + 1) for i in range(1, parts - 1, 2)] + [(i + 1, i) for i in range(1, parts - 1, 2)]
    inner_pairs = [(i, i ^ 1) for i in range(parts)]
    near = [(i, i ^ 1) for i in range(4)]
    far = [(i, i ^ 2) for i in range(4)]
    cross = [(m * parts + i, (m ^ 3) * parts + j) for m in range(4) for i, j in outer_pairs]
    links = face_links
    side = odd.reshape(1)
    rims = jnp.concatenate([traces[:, :HALO], traces[:, OWN - HALO :]], axis=1)
    inside = traces[:, HALO : OWN - HALO]
    x2a = lax.ppermute(rims, "mode", far)
    x1 = lax.ppermute(traces, "mode", near)
    g0 = gather_own(side, links, rims, inside)
    to_far, g0 = lax.optimization_barrier((inside, g0))
    x2b = lax.ppermute(to_far, "mode", far)
    to_outer = lax.dynamic_slice_in_dim(jnp.concatenate([rims, x2a], axis=0), HALO * odd, HALO, axis=1)
    o31 = lax.ppermute(to_outer, ("mode", "space"), cross)
    x3a = lax.ppermute(x2a, "mode", near)
    x3b = lax.ppermute(x2b, "mode", near)
    o20 = lax.ppermute(o31, "mode", near)
    near_rims = jnp.concatenate([x1[:, :HALO], x1[:, OWN - HALO :]], axis=1)
    all_rims = jnp.concatenate([x3a, near_rims, x2a, rims], axis=0)
    inner = lax.ppermute(lax.dynamic_slice_in_dim(all_rims, HALO * (1 - odd), HALO, axis=1), "space", inner_pairs)
    table = coupling_table(me, pair_modes, pair_terms, pair_values)
    g1 = gather_own(side, links, x1)
    g2 = gather_own(side, links, x2a, x2b)
    g3 = gather_own(side, links, x3a, x3b)
    ha = gather_halo(side, links, o31, inner, 0)
    hb = gather_halo(side, links, o20, inner, 1)
    local, to_back, to_sibling = elements(side, (g0, g1, g2, g3), (ha, hb), table, elem_mats, links)
    back_outer = lax.ppermute(to_back, "space", outer_pairs)
    back_inner = lax.ppermute(to_sibling, "space", inner_pairs)
    own = scatter_own(side, local, links)
    return finish(side, own, back_outer, back_inner)


def solution(mesh):
    return jax.shard_map(
        body,
        mesh=mesh,
        in_specs=(P("mode", "space"), P(None, None, "space"), P(None, "space"), P(), P(), P()),
        out_specs=P("mode", "space"),
        check_vma=False,
    )
```

```python
import functools

import jax
import jax.numpy as jnp
from jax import lax
from jax.experimental import pallas as pl
from jax.experimental.pallas import tpu as pltpu
from jax.sharding import PartitionSpec as P


HALO = 512
MD = 30
SLOTS = 6
E = 1024
OWN = 3072
TERMS = 4
LANES = SLOTS * E
NN = (((1,), (0,)), ((), ()))
NT = (((1,), (1,)), ((), ()))
F32 = jnp.float32
BF16 = jnp.bfloat16
STEP = 512
VMEM = pl.BlockSpec(memory_space=pltpu.VMEM)
PARAMS = pltpu.CompilerParams(vmem_limit_bytes=16 << 20)
ELEMENT_PARAMS = pltpu.CompilerParams(vmem_limit_bytes=16 << 20)


def split_hi_lo(x):
    hi = x.astype(BF16)
    lo = (x - hi.astype(F32)).astype(BF16)
    return hi, lo


def codes(links, odd):
    own = links - HALO
    mine = jnp.where(own < HALO, own, jnp.where(own < OWN - HALO, own + HALO, own - (OWN - 2 * HALO)))
    left = links + OWN + HALO * odd
    right = links - HALO * odd
    faces = jnp.where(links < HALO, left, jnp.where(links < HALO + OWN, mine, right))
    return faces >> 10, (faces >> 8) & 3, faces & 255


def one_hot(chunk_of, row, chunk):
    n = row.shape[1]
    ids = lax.broadcasted_iota(jnp.int32, (256, n), 0).astype(F32).astype(BF16)
    mine = jnp.where(chunk_of == chunk, row, -1).astype(F32).astype(BF16)
    return jnp.where(ids == mine, jnp.ones((), BF16), jnp.zeros((), BF16))


def fill(piece, t_ref, base, lane):
    n = piece.shape[0]
    hi, lo = split_hi_lo(piece)
    t_ref[base : base + n, lane : lane + 256] = hi
    t_ref[base + 32 : base + 32 + n, lane : lane + 256] = lo


def pick(got, quad):
    total = jnp.zeros((64, got.shape[1]), F32)
    for q in range(4):
        total = total + jnp.where(quad == q, got[q * 64 : (q + 1) * 64], 0.0)
    return total.astype(BF16)


def table_kernel(me_ref, modes_ref, terms_ref, values_ref, out_ref, ids_ref, v_ref):
    me = me_ref[0]
    n = values_ref.shape[0]
    wide = v_ref.shape[1]
    ids_ref[...] = jnp.full(ids_ref.shape, -1, jnp.int32)
    v_ref[...] = jnp.zeros(v_ref.shape, F32)
    v_ref[0, 0:n] = values_ref[...]
    ids_ref[2, 0:n] = terms_ref[...]
    i_loc = modes_ref[0:1, :] - MD * me
    ids_ref[0:1, 0:n] = jnp.where((i_loc >= 0) & (i_loc < MD), ids_ref[2:3, 0:n] * 32 + i_loc, -1)
    j = modes_ref[1:2, :]
    part = (j >= MD).astype(jnp.int32) + (j >= 2 * MD).astype(jnp.int32) + (j >= 3 * MD).astype(jnp.int32)
    ids_ref[1:2, 0:n] = (part ^ me) * 64 + (j - MD * part)
    rid = lax.broadcasted_iota(jnp.int32, (128, wide), 0)
    cid = lax.broadcasted_iota(jnp.int32, (256, wide), 0)
    cols = jnp.where((cid & ~32) == ids_ref[1:2, :], 1.0, 0.0).astype(BF16)
    left = jnp.where(rid == ids_ref[0:1, :], v_ref[0:1, :], 0.0)
    a = left.astype(BF16)
    rest = left - a.astype(F32)
    b = rest.astype(BF16)
    c = (rest - b.astype(F32)).astype(BF16)
    total = lax.dot_general(a, cols, NT, preferred_element_type=F32)
    total = total + lax.dot_general(b, cols, NT, preferred_element_type=F32)
    total = total + lax.dot_general(c, cols, NT, preferred_element_type=F32)
    hi, lo = split_hi_lo(total)
    out_ref[0:128, :] = hi
    out_ref[128:256, :] = lo


SMEM = pl.BlockSpec(memory_space=pltpu.SMEM)


def coupling_table(me, pair_modes, pair_terms, pair_values):
    n = pair_values.shape[0]
    wide = -(-n // 128) * 128
    return pl.pallas_call(
        table_kernel,
        out_shape=jax.ShapeDtypeStruct((256, 256), BF16),
        in_specs=[SMEM] + [VMEM] * 3,
        out_specs=VMEM,
        scratch_shapes=[pltpu.VMEM((8, wide), jnp.int32), pltpu.VMEM((8, wide), F32)],
        compiler_params=PARAMS,
    )(me, pair_modes, pair_terms, pair_values)


def gather_body(piece, odd_ref, links_ref, out_ref, t_ref):
    for r in range(8):
        t_ref[r * 32 + 16 : r * 32 + 32, :] = jnp.zeros((16, 768), BF16)
    for c in range(3):
        for q in range(4):
            fill(piece(c, q), t_ref, q * 64, c * 256)
    for b in range(SLOTS):
        chunk_of, quad, row = codes(links_ref[b : b + 1, :], odd_ref[0])
        hot = jnp.concatenate([one_hot(chunk_of, row, c) for c in range(3)], axis=0)
        got = lax.dot_general(t_ref[...], hot, NN, preferred_element_type=F32)
        out_ref[:, b * E : (b + 1) * E] = pick(got, jnp.where(chunk_of < 3, quad, -1))


def gather_whole_kernel(odd_ref, x_ref, links_ref, out_ref, t_ref):
    def piece(c, q):
        first = HALO + (c - 1) * 1024 + q * 256 if c else q * 256 + (q // 2) * (OWN - 2 * HALO)
        return x_ref[:, first : first + 256]

    gather_body(piece, odd_ref, links_ref, out_ref, t_ref)


def gather_parts_kernel(odd_ref, rims_ref, inside_ref, links_ref, out_ref, t_ref):
    def piece(c, q):
        first = (c - 1) * 1024 + q * 256
        return inside_ref[:, first : first + 256] if c else rims_ref[:, q * 256 : (q + 1) * 256]

    gather_body(piece, odd_ref, links_ref, out_ref, t_ref)


def gather_own(odd, links, *xs):
    return pl.pallas_call(
        gather_whole_kernel if len(xs) == 1 else gather_parts_kernel,
        out_shape=jax.ShapeDtypeStruct((64, LANES), BF16),
        in_specs=[SMEM] + [VMEM] * (len(xs) + 1),
        out_specs=VMEM,
        scratch_shapes=[pltpu.VMEM((256, 768), BF16)],
        compiler_params=PARAMS,
    )(odd, *xs, links)


def gather_halo_kernel(half, odd_ref, outer_ref, inner_ref, links_ref, out_ref, t_ref):
    for r in range(16):
        t_ref[r * 32 + 16 : r * 32 + 32, :] = jnp.zeros((16, 256), BF16)
    for d in range(2):
        for q in range(2):
            here = slice(q * 256, (q + 1) * 256)
            fill(outer_ref[d * MD : (d + 1) * MD, here], t_ref, (d * 4 + q) * 64, 0)
            first = (2 * half + d) * MD
            fill(inner_ref[first : first + MD, here], t_ref, (d * 4 + 2 + q) * 64, 0)
    for b in range(SLOTS):
        chunk_of, quad, row = codes(links_ref[b : b + 1, :], odd_ref[0])
        hot = one_hot(chunk_of, row, 3)
        for d in range(2):
            got = lax.dot_general(t_ref[d * 256 : (d + 1) * 256, :], hot, NN, preferred_element_type=F32)
            out_ref[d * 64 : (d + 1) * 64, b * E : (b + 1) * E] = pick(got, quad)


def gather_halo(odd, links, outer, inner, half):
    return pl.pallas_call(
        functools.partial(gather_halo_kernel, half),
        out_shape=jax.ShapeDtypeStruct((128, LANES), BF16),
        in_specs=[SMEM] + [VMEM] * 3,
        out_specs=VMEM,
        scratch_shapes=[pltpu.VMEM((512, 256), BF16)],
        compiler_params=PARAMS,
    )(odd, outer, inner, links)


def scatter_chunk(odd_ref, l_ref, links_ref, chunk):
    total = None
    for a in range(SLOTS):
        chunk_of, _, row = codes(links_ref[a : a + 1, :], odd_ref[0])
        hot = one_hot(chunk_of, row, chunk)
        part = lax.dot_general(l_ref[:, a * E : (a + 1) * E], hot, NT, preferred_element_type=F32)
        total = part if total is None else total + part
    return total


def element_kernel(odd_ref, g0, g1, g2, g3, ha, hb, table_ref, mats_ref, links_ref, l_ref, outer_ref, inner_ref, y_ref):
    total = None
    for base in range(0, E, STEP):
        for b in range(SLOTS):
            here = slice(b * E + base, b * E + base + STEP)
            right = jnp.concatenate(
                [
                    g0[:, here] + hb[64:128, here],
                    g1[:, here] + ha[64:128, here],
                    g2[:, here] + hb[0:64, here],
                    g3[:, here] + ha[0:64, here],
                ],
                axis=0,
            )
            got = lax.dot_general(table_ref[...], right, NN, preferred_element_type=F32)
            own = right[0:64].astype(F32)
            y_ref[b, 0:32] = own[0:32] + own[32:64]
            y_ref[b, 32:160] = got[0:128] + got[128:256]
        for first in range(0, SLOTS, 2):
            slots = (first, first + 1)
            for lane in range(0, STEP, 256):
                here = slice(base + lane, base + lane + 256)
                acc = [None, None]
                for b in range(SLOTS):
                    for k in range(TERMS + 1):
                        y = y_ref[b, 32 * k : 32 * (k + 1), lane : lane + 256]
                        for i, a in enumerate(slots):
                            term = mats_ref[k, 6 * a + b : 6 * a + b + 1, here] * y
                            acc[i] = term if acc[i] is None else acc[i] + term
                for i, a in enumerate(slots):
                    _, quad, _ = codes(links_ref[a : a + 1, here], odd_ref[0])
                    hi = acc[i].astype(BF16).astype(F32)
                    lo = acc[i] - hi
                    there = slice(a * E + base + lane, a * E + base + lane + 256)
                    for q in range(4):
                        l_ref[q * 64 : q * 64 + 32, there] = jnp.where(quad == q, hi, 0.0).astype(BF16)
                        l_ref[q * 64 + 32 : q * 64 + 64, there] = jnp.where(quad == q, lo, 0.0).astype(BF16)
            for a in slots:
                chunk_of, _, row = codes(links_ref[a : a + 1, base : base + STEP], odd_ref[0])
                hot = one_hot(chunk_of, row, 3)
                there = slice(a * E + base, a * E + base + STEP)
                part = lax.dot_general(l_ref[:, there], hot, NT, preferred_element_type=F32)
                total = part if total is None else total + part
    for q in range(4):
        both = total[q * 64 : q * 64 + 32] + total[q * 64 + 32 : q * 64 + 64]
        ref = inner_ref if q // 2 else outer_ref
        ref[:, (q % 2) * 256 : (q % 2 + 1) * 256] = both[0:MD]


def elements(odd, gs, halos, table, mats, links):
    rim = jax.ShapeDtypeStruct((MD, HALO), F32)
    return pl.pallas_call(
        element_kernel,
        out_shape=(jax.ShapeDtypeStruct((256, LANES), BF16), rim, rim),
        in_specs=[SMEM] + [VMEM] * 9,
        out_specs=(VMEM, VMEM, VMEM),
        scratch_shapes=[pltpu.VMEM((SLOTS, 160, STEP), F32)],
        compiler_params=ELEMENT_PARAMS,
    )(odd, *gs, *halos, table, mats, links)


def own_kernel(odd_ref, l_ref, links_ref, out_ref):
    for chunk in range(3):
        total = scatter_chunk(odd_ref, l_ref, links_ref, chunk)
        for q in range(4):
            both = total[q * 64 : q * 64 + 32] + total[q * 64 + 32 : q * 64 + 64]
            first = HALO + (chunk - 1) * 1024 + q * 256 if chunk else q * 256 + (q // 2) * (OWN - 2 * HALO)
            out_ref[:, first : first + 256] = both[0:MD]


def scatter_own(odd, l, links):
    return pl.pallas_call(
        own_kernel,
        out_shape=jax.ShapeDtypeStruct((MD, OWN), F32),
        in_specs=[SMEM] + [VMEM] * 2,
        out_specs=VMEM,
        compiler_params=PARAMS,
    )(odd, l, links)


def finish_kernel(odd_ref, own_ref, out_in_ref, in_in_ref, out_ref):
    odd = odd_ref[0] == 1
    outer = out_in_ref[...]
    inner = in_in_ref[...]
    out_ref[:, HALO : OWN - HALO] = own_ref[:, HALO : OWN - HALO]
    out_ref[:, :HALO] = own_ref[:, :HALO] + jnp.where(odd, inner, outer)
    out_ref[:, OWN - HALO :] = own_ref[:, OWN - HALO :] + jnp.where(odd, outer, inner)


def finish(odd, own, outer, inner):
    return pl.pallas_call(
        finish_kernel,
        out_shape=jax.ShapeDtypeStruct((MD, OWN), F32),
        in_specs=[pl.BlockSpec(memory_space=pltpu.SMEM)] + [VMEM] * 3,
        out_specs=VMEM,
        compiler_params=PARAMS,
    )(odd, own, outer, inner)


def body(traces, elem_mats, face_links, pair_modes, pair_terms, pair_values):
    parts = lax.axis_size("space")
    me = lax.axis_index("mode").astype(jnp.int32).reshape(1)
    odd = lax.axis_index("space").astype(jnp.int32) % 2
    outer_pairs = [(i, i + 1) for i in range(1, parts - 1, 2)] + [(i + 1, i) for i in range(1, parts - 1, 2)]
    inner_pairs = [(i, i ^ 1) for i in range(parts)]
    near = [(i, i ^ 1) for i in range(4)]
    far = [(i, i ^ 2) for i in range(4)]
    cross = [(m * parts + i, (m ^ 3) * parts + j) for m in range(4) for i, j in outer_pairs]
    links = face_links
    side = odd.reshape(1)
    rims = jnp.concatenate([traces[:, :HALO], traces[:, OWN - HALO :]], axis=1)
    inside = traces[:, HALO : OWN - HALO]
    x2a = lax.ppermute(rims, "mode", far)
    x1 = lax.ppermute(traces, "mode", near)
    g0 = gather_own(side, links, rims, inside)
    to_far, g0 = lax.optimization_barrier((inside, g0))
    x2b = lax.ppermute(to_far, "mode", far)
    to_outer = lax.dynamic_slice_in_dim(jnp.concatenate([rims, x2a], axis=0), HALO * odd, HALO, axis=1)
    o31 = lax.ppermute(to_outer, ("mode", "space"), cross)
    x3a = lax.ppermute(x2a, "mode", near)
    x3b = lax.ppermute(x2b, "mode", near)
    o20 = lax.ppermute(o31, "mode", near)
    near_rims = jnp.concatenate([x1[:, :HALO], x1[:, OWN - HALO :]], axis=1)
    all_rims = jnp.concatenate([x3a, near_rims, x2a, rims], axis=0)
    inner = lax.ppermute(lax.dynamic_slice_in_dim(all_rims, HALO * (1 - odd), HALO, axis=1), "space", inner_pairs)
    table = coupling_table(me, pair_modes, pair_terms, pair_values)
    g1 = gather_own(side, links, x1)
    g2 = gather_own(side, links, x2a, x2b)
    g3 = gather_own(side, links, x3a, x3b)
    ha = gather_halo(side, links, o31, inner, 0)
    hb = gather_halo(side, links, o20, inner, 1)
    local, to_back, to_sibling = elements(side, (g0, g1, g2, g3), (ha, hb), table, elem_mats, links)
    back_outer = lax.ppermute(to_back, "space", outer_pairs)
    back_inner = lax.ppermute(to_sibling, "space", inner_pairs)
    own = scatter_own(side, local, links)
    return finish(side, own, back_outer, back_inner)


def solution(mesh):
    return jax.shard_map(
        body,
        mesh=mesh,
        in_specs=(P("mode", "space"), P(None, None, "space"), P(None, "space"), P(), P(), P()),
        out_specs=P("mode", "space"),
        check_vma=False,
    )
```
